32 devices in a mesh: parts: 2 (over x), leaf: 16 (over z, y, core).
Axes of the slice: x: 2, y: 2, z: 4, core: 2. Of those that a mesh axis runs over, the one named last changes fastest.
Arguments:
- right_sides: bfloat16 [128, 16384], P('parts', 'leaf'), parts along dimension 0, may hold values from -6 to 6
- near_list: int32 [32, 3], P(('parts', 'leaf')), parts along dimension 0, may hold values from 0 to 15, as said below
- near_blocks: bfloat16 [32, 3, 1024, 1024], P(('parts', 'leaf')), parts along dimension 0, may hold values from -0.02734375 to 0.02734375
- inverse_list: int32 [32, 2], P(('parts', 'leaf')), parts along dimension 0, may hold values from 0 to 15, as said below
- inverse_blocks: bfloat16 [32, 2, 1024, 1024], P(('parts', 'leaf')), parts along dimension 0, may hold values from -0.03125 to 0.03125
- leaf_bases: bfloat16 [32, 1024, 128], P(('parts', 'leaf')), parts along dimension 0, may hold values from -0.1875 to 0.1875
- transfers: bfloat16 [2, 2, 128, 128], replicated, may hold values from -0.375 to 0.375
- couple_list: int32 [32, 3, 4], P(('parts', 'leaf')), parts along dimension 0, may hold values from 0 to 15, as said below
- couple_blocks: bfloat16 [32, 3, 4, 128, 128], P(('parts', 'leaf')), parts along dimension 0, may hold values from -0.125 to 0.125
Outputs:
- solution: float32 [128, 16384], P('parts', 'leaf'), parts along dimension 0
- residual: float32 [128, 16384], P('parts', 'leaf'), parts along dimension 0
The draws below stay inside these ranges and needn't reach their ends.
There are 2 independent parts, one for each index of `parts`. The reference program is written for one: setup_inputs(seed, part) draws one part's arguments, and reference() takes and returns one part's arrays. A program takes and returns all parts, laid end to end along the dimension named above; an argument that names none is the same for every part. Nothing has to cross between parts.
Inputs may be any that keep to these rules, and one draw needn't show every extreme that they name: `near_list`: entry [i, s] lies within 2 of i. `inverse_list`: entry [i, s] lies within 2 of i. `couple_list`: entry [i, l, k] names a cluster of level l, below 16 // 2 ** l.
All inputs are finite; a program needn't handle non-finite values.
Results may differ from the reference program's by a relative error of at most 0.014.
Values may be sent and summed in bfloat16 or wider, within the bound.
A program may use at most 64 MiB of HBM per device.

```python
import jax
import jax.numpy as jnp
from jax import lax

LEAF = 1024
RANK = 128
RHS = 64
NEAR = 3
SAI = 2
REACH = 2
PARTNERS = 4
LEVELS = 3
LEAVES = 16
ROWS = 16384


def bounded_partners(key, count):
    first_key, second_key = jax.random.split(key)
    offsets = jax.random.randint(first_key, (LEAVES, count), -REACH, REACH + 1)
    center_leaf = jax.random.randint(second_key, (), REACH, LEAVES - REACH)
    row_index = jnp.arange(LEAVES, dtype=jnp.int32)[:, None]
    slot_index = jnp.arange(count, dtype=jnp.int32)[None, :]
    chosen_row = row_index == center_leaf
    offsets = jnp.where(chosen_row & (slot_index == 0), -REACH, offsets)
    offsets = jnp.where(chosen_row & (slot_index == 1), REACH, offsets)
    return jnp.clip(row_index + offsets, 0, LEAVES - 1).astype(jnp.int32)


def draw_near_list(key, part):
    return bounded_partners(jax.random.fold_in(key, 11), NEAR)


def draw_inverse_list(key, part):
    return bounded_partners(jax.random.fold_in(key, 23), SAI)


def draw_couple_list(key, part):
    limits = jnp.array([LEAVES, LEAVES // 2, LEAVES // 4], jnp.int32)[None, :, None]
    drawn = jax.random.randint(jax.random.fold_in(key, 37), (LEAVES, LEVELS, PARTNERS), 0, limits)
    divisors = jnp.array([1, 2, 4], jnp.int32)[None, :]
    row_index = jnp.arange(LEAVES, dtype=jnp.int32)[:, None]
    named = (row_index // divisors + 1) % limits[:, :, 0]
    slot_index = jnp.arange(PARTNERS, dtype=jnp.int32)[None, None, :]
    drawn = jnp.where(slot_index == 0, named[:, :, None], drawn)
    return drawn.astype(jnp.int32)


def levels(key, extent, cuts, smallest, high):
    def one(dim, blocks):
        heights = jax.random.uniform(jax.random.fold_in(jax.random.fold_in(key, 6), dim), (blocks,), jnp.float32, smallest / len(cuts), high / len(cuts))
        return jnp.repeat(jnp.exp(heights), extent[dim] // blocks).reshape((-1,) + (1,) * (len(extent) - dim - 1))

    loudness = one(*cuts[0])
    for cut in cuts[1:]:
        loudness = loudness * one(*cut)
    return loudness


def gaussian(rng, dims, scale, reach, cuts=(), held_as=jnp.bfloat16):
    entries = scale * jax.random.normal(rng, dims, jnp.float32)
    if cuts:
        entries = entries * levels(rng, dims, cuts, -0.22, 0.18)
    return jnp.clip(entries, -reach, reach).astype(held_as)


def setup_inputs(seed: int = 0, part: int = 0) -> dict:
    keys = jax.random.split(jax.random.key(seed), 10)
    own_keys = jax.random.split(jax.random.fold_in(keys[9], part), 10)
    return {
        "right_sides": gaussian(own_keys[0], (RHS, ROWS), 1.0, 6.0, ((1, 16),)),
        "near_list": draw_near_list(jax.random.fold_in(jax.random.fold_in(keys[9], part), 71), part),
        "near_blocks": gaussian(own_keys[2], (LEAVES, NEAR, LEAF, LEAF), (16 * NEAR * LEAF) ** -0.5, 0.02734375, ((0, 16),)),
        "inverse_list": draw_inverse_list(jax.random.fold_in(jax.random.fold_in(keys[9], part), 71), part),
        "inverse_blocks": gaussian(own_keys[4], (LEAVES, SAI, LEAF, LEAF), (16 * SAI * LEAF) ** -0.5, 0.03125, ((0, 16),)),
        "leaf_bases": gaussian(own_keys[5], (LEAVES, LEAF, RANK), LEAF ** -0.5, 0.1875, ((0, 16),)),
        "transfers": gaussian(keys[6], (2, 2, RANK, RANK), (2 * RANK) ** -0.5, 0.375),
        "couple_list": draw_couple_list(jax.random.fold_in(jax.random.fold_in(keys[9], part), 71), part),
        "couple_blocks": gaussian(own_keys[8], (LEAVES, LEVELS, PARTNERS, RANK, RANK), (4 * PARTNERS * RANK) ** -0.5, 0.125, ((0, 16),)),
    }


exact_mode = lax.Precision.HIGHEST


def to_half(values):
    return lax.optimization_barrier(values.astype(jnp.bfloat16))


def leaf_major(vectors):
    return jnp.transpose(vectors.reshape(vectors.shape[0], LEAVES, LEAF), (1, 0, 2))


def apply_blocks(vectors, partner_lists, blocks):
    grouped = leaf_major(vectors)

    def one_leaf(leaf_index):
        running = jnp.zeros(grouped.shape[1:], jnp.float32)
        for slot_index in range(partner_lists.shape[1]):
            partner = partner_lists[leaf_index, slot_index]
            chosen = lax.dynamic_index_in_dim(grouped, partner, 0, keepdims=False)
            running = running + jnp.dot(chosen, blocks[leaf_index, slot_index], preferred_element_type=jnp.float32)
        return running

    outcome = lax.map(one_leaf, jnp.arange(LEAVES, dtype=jnp.int32))
    return jnp.transpose(outcome, (1, 0, 2)).reshape(vectors.shape[0], LEAVES * LEAF)


def lift(coeffs, child_maps):
    grouped = coeffs.reshape(coeffs.shape[0] // 2, 2, coeffs.shape[1], coeffs.shape[2]).astype(jnp.float32)
    left_part = jnp.einsum("prs,st->prt", grouped[:, 0], child_maps[0].astype(jnp.float32), precision=exact_mode)
    right_part = jnp.einsum("prs,st->prt", grouped[:, 1], child_maps[1].astype(jnp.float32), precision=exact_mode)
    return to_half(left_part + right_part)


def descend(coarse, lower_count, child_maps):
    parity = jnp.arange(lower_count, dtype=jnp.int32) % 2
    spread = jnp.repeat(coarse, 2, axis=0)
    chosen = child_maps[parity].astype(jnp.float32)
    return jnp.einsum("prs,pts->prt", spread, chosen, precision=exact_mode)


def far_field(vectors, leaf_bases, transfers, couple_list, couple_blocks):
    grouped = leaf_major(vectors).astype(jnp.float32)
    bases_wide = leaf_bases.astype(jnp.float32)
    coeff_zero = to_half(jnp.einsum("lrj,ljs->lrs", grouped, bases_wide, precision=exact_mode))
    coeff_one = lift(coeff_zero, transfers[0])
    coeff_two = lift(coeff_one, transfers[1])
    fields = []
    for tree_level, coeff_table in enumerate((coeff_zero, coeff_one, coeff_two)):
        chosen = coeff_table[couple_list[:, tree_level]].astype(jnp.float32)
        level_blocks = couple_blocks[:, tree_level].astype(jnp.float32)
        fields.append(jnp.einsum("lkrs,lkst->lrt", chosen, level_blocks, precision=exact_mode))
    pair_one = fields[1][0::2] + fields[1][1::2]
    pair_two = fields[2][0::2] + fields[2][1::2]
    quad_sum = pair_two[0::2] + pair_two[1::2]
    down_one = pair_one + descend(quad_sum, LEAVES // 2, transfers[1])
    leaf_field = fields[0] + descend(down_one, LEAVES, transfers[0])
    rounded = to_half(leaf_field).astype(jnp.float32)
    outcome = jnp.einsum("lrs,ljs->lrj", rounded, bases_wide, precision=exact_mode)
    return jnp.transpose(outcome, (1, 0, 2)).reshape(vectors.shape[0], LEAVES * LEAF)


def reference(right_sides, near_list, near_blocks, inverse_list, inverse_blocks, leaf_bases, transfers, couple_list, couple_blocks):
    def operate(half_vector):
        near_part = apply_blocks(half_vector, near_list, near_blocks)
        far_part = far_field(half_vector, leaf_bases, transfers, couple_list, couple_blocks)
        return half_vector.astype(jnp.float32) + near_part + far_part

    def precondition(half_vector):
        return half_vector.astype(jnp.float32) + apply_blocks(half_vector, inverse_list, inverse_blocks)

    wide_sides = right_sides.astype(jnp.float32)
    iterate_one = precondition(right_sides)
    residual_one = wide_sides - operate(to_half(iterate_one))
    solution = iterate_one + precondition(to_half(residual_one))
    residual = wide_sides - operate(to_half(solution))
    return solution, residual
```

```python
import functools

import jax
import jax.numpy as jnp
from jax import lax
from jax.experimental import pallas as pl
from jax.experimental.pallas import tpu as pltpu
from jax.sharding import PartitionSpec as P

REACH = 2
CHUNKS = 4
EXCHANGES = 4
OWN_SIB, OWN_PAIR, FWD_QUAD, FWD_SIB = range(4)
F32 = jnp.float32
BF16 = jnp.bfloat16


def mm(a, b):
    return jnp.dot(a, b, preferred_element_type=F32)


def mm_t(a, b):
    return lax.dot_general(a, b, (((1,), (1,)), ((), ())), preferred_element_type=F32)


def kernel(
    count,
    near_list,
    inverse_list,
    couple_list,
    sides_hbm,
    near_hbm,
    inverse_hbm,
    bases_hbm,
    transfers_hbm,
    couple_hbm,
    sol_ref,
    res_ref,
    *scratch,
):
    windows = [scratch[e * CHUNKS : (e + 1) * CHUNKS] for e in range(EXCHANGES)]
    (
        tables_a,
        tables_b,
        got_a,
        got_b,
        mine_a,
        mine_b,
        level_one,
        level_two,
        near,
        inverse,
        bases,
        transfers,
        couple,
        acc,
        load_sem,
        sides_sem,
        send_sem,
        recv_sem,
        far_send,
        far_recv,
        step_send,
        step_recv,
    ) = scratch[EXCHANGES * CHUNKS :]
    tables = (tables_a, tables_b)
    got = (got_a, got_b)
    mine = (mine_a, mine_b)
    quads = count // 4
    rows, cols = sol_ref.shape
    width = cols // CHUNKS

    me = lax.axis_index("leaf")
    core = me % 2
    odd = me // 2 % 2
    member = me % 4
    quad = me // 4
    sibling = me + 1 - 2 * core
    pair = me + 2 - 4 * odd
    across = pair + 1 - 2 * core
    pair_slot = 4 - 4 * odd
    fwd_slot = 4 * odd
    pair_dst_slot = 4 * odd
    fwd_to = me + 4 - 8 * odd
    fwd_out = (fwd_to >= 0) & (fwd_to < count)
    fwd_from = me - 4 + 8 * odd
    fwd_in = (fwd_from >= 0) & (fwd_from < count)
    same = core == odd

    sides_loads = []
    for c in range(CHUNKS):
        load = pltpu.make_async_copy(
            sides_hbm.at[:, pl.ds(c * width, width)], windows[0][c].at[2], sides_sem.at[c]
        )
        load.start()
        sides_loads.append(load)
    loads = {}
    pieces = []
    for s in range(inverse.shape[0]):
        pieces.append(("inverse%d" % s, inverse_hbm.at[0, s], inverse.at[s]))
    pieces.append(("bases", bases_hbm.at[0], bases))
    pieces.append(("transfers", transfers_hbm, transfers))
    pieces.append(("couple", couple_hbm.at[0], couple))
    for s in range(near.shape[0]):
        pieces.append(("near%d" % s, near_hbm.at[0, s], near.at[s]))
    for index, (name, source, target) in enumerate(pieces):
        loads[name] = pltpu.make_async_copy(source, target, load_sem.at[index])
        loads[name].start()

    def wait_load(*names):
        for name in names:
            if name in loads:
                loads.pop(name).wait()

    barrier = pltpu.get_barrier_semaphore()
    partners = [sibling, pair, across]
    partners += [(quad + k) % quads * 4 + member for k in range(1, quads)]
    for other in partners:
        pl.semaphore_signal(
            barrier, inc=1, device_id={"leaf": other}, device_id_type=pl.DeviceIdType.MESH
        )
    pl.semaphore_wait(barrier, len(partners))

    unsent = []

    def remote(src, dst, ssem, rsem, to):
        return pltpu.make_async_remote_copy(
            src_ref=src,
            dst_ref=dst,
            send_sem=ssem,
            recv_sem=rsem,
            device_id={"leaf": to},
            device_id_type=pl.DeviceIdType.MESH,
        )

    def vector_copy(e, c, kind):
        win = windows[e][c]
        if kind == OWN_SIB:
            src, dst, to = 2, 1 + 2 * core, sibling
            dst = jnp.where(core == 0, 1, 3)
        elif kind == OWN_PAIR:
            src, dst, to = 2, pair_dst_slot, pair
        elif kind == FWD_QUAD:
            src, dst, to = pair_slot, fwd_slot, fwd_to
        else:
            src, dst, to = 4 - 4 * core, 3 - 2 * core, sibling
        return remote(
            win.at[src], win.at[dst], send_sem.at[e, kind, c], recv_sem.at[e, kind, c], to
        )

    def start(e, c, kind, pred=None):
        if pred is None:
            vector_copy(e, c, kind).start()
        else:
            pl.when(pred)(lambda: vector_copy(e, c, kind).start())

    def wait_recv(e, c, kind, pred=None):
        if pred is None:
            vector_copy(e, c, kind).wait_recv()
        else:
            pl.when(pred)(lambda: vector_copy(e, c, kind).wait_recv())

    def send_own(e, c):
        start(e, c, OWN_PAIR)
        start(e, c, OWN_SIB)

    def relay(e, c):
        wait_recv(e, c, OWN_PAIR)
        start(e, c, FWD_QUAD, fwd_out)
        start(e, c, FWD_SIB, same)
        wait_recv(e, c, FWD_QUAD, fwd_in)
        start(e, c, FWD_SIB, jnp.logical_not(same) & fwd_in)

    def arrive(e, c):
        wait_recv(e, c, OWN_SIB)
        wait_recv(e, c, FWD_SIB, jnp.logical_not(same) | fwd_in)

    def drain(e):
        for c in range(CHUNKS):
            vector_copy(e, c, OWN_PAIR).wait_send()
            vector_copy(e, c, OWN_SIB).wait_send()
            pl.when(fwd_out)(lambda c=c: vector_copy(e, c, FWD_QUAD).wait_send())
            pl.when(same | fwd_in)(lambda c=c: vector_copy(e, c, FWD_SIB).wait_send())

    def own(e):
        return jnp.concatenate([windows[e][c][2] for c in range(CHUNKS)], axis=1)

    def put_own(e, value):
        for c in range(CHUNKS):
            windows[e][c][2] = value[:, c * width : (c + 1) * width].astype(BF16)
            send_own(e, c)

    def within(leaf):
        return jnp.clip(leaf - me + REACH, 0, 2 * REACH)

    near_at = [within(near_list[0, s]) for s in range(near.shape[0])]
    inverse_at = [within(inverse_list[0, s]) for s in range(inverse.shape[0])]

    def slots(e, c, at, blocks, label):
        arrive(e, c)
        total = None
        for s, position in enumerate(at):
            wait_load("%s%d" % (label, s))
            chosen = windows[e][c][position]
            term = mm(chosen, blocks[s, c * width : (c + 1) * width, :])
            total = term if total is None else total + term
        if c == 0:
            acc[...] = total
        else:
            acc[...] += total

    def blocksum(e, at, blocks, label):
        relay(e, 0)
        for c in range(CHUNKS):
            if c + 1 < CHUNKS:
                relay(e, c + 1)
            slots(e, c, at, blocks, label)

    def far_along(a, k):
        ref = tables[a].at[member, quad]
        return remote(ref, ref, far_send.at[a, k], far_recv.at[a, k], (quad + k) % quads * 4 + member)

    def far_step(a, kind):
        table = tables[a]
        if kind == 0:
            ref, to, dst = table.at[member], pair, None
        elif kind == 1:
            ref, to, dst = table.at[member], sibling, None
        elif kind == 2:
            ref, to, dst = table.at[pair % 4], sibling, None
        elif kind == 3:
            ref, to, dst = mine[a], sibling, got[a].at[pl.ds(0, 2)]
        elif kind == 4:
            ref, to, dst = mine[a].at[1], pair, got[a].at[2]
        else:
            ref, to, dst = mine[a].at[1], across, got[a].at[3]
        return remote(
            ref, ref if dst is None else dst, step_send.at[a, kind], step_recv.at[a, kind], to
        )

    def far_begin(a, e):
        wait_load("bases")
        tables[a][member, quad] = mm(own(e), bases[...]).astype(BF16)
        for k in range(1, quads):
            far_along(a, k).start()

    def far_mid(a):
        for k in range(1, quads):
            far_along(a, k).wait_recv()
        far_step(a, 0).start()
        far_step(a, 1).start()

    def far_late(a):
        far_step(a, 0).wait_recv()
        far_step(a, 2).start()

    def far_couple(a):
        table = tables[a]
        wait_load("transfers", "couple")
        far_step(a, 1).wait_recv()
        far_step(a, 2).wait_recv()
        rank = table.shape[-1]
        flat = (quads * rows, rank)
        for parity in range(2):
            lifted = mm(table[2 * parity].reshape(flat), transfers[0, 0])
            lifted = lifted + mm(table[2 * parity + 1].reshape(flat), transfers[0, 1])
            level_one[parity] = lifted.astype(BF16).reshape(quads, rows, rank)
        lifted = mm(level_one[0].reshape(flat), transfers[1, 0])
        lifted = lifted + mm(level_one[1].reshape(flat), transfers[1, 1])
        level_two[...] = lifted.astype(BF16).reshape(quads, rows, rank)
        fields = []
        for level in range(3):
            total = None
            for k in range(couple.shape[1]):
                at = couple_list[level, 0, k]
                if level == 0:
                    chosen = table[at % 4, at // 4]
                elif level == 1:
                    chosen = level_one[at % 2, at // 2]
                else:
                    chosen = level_two[at]
                term = mm(chosen, couple[level, k])
                total = term if total is None else total + term
            fields.append(total)
        mine[a][0] = fields[1].astype(BF16)
        mine[a][1] = fields[2].astype(BF16)
        for kind in (4, 5, 3):
            far_step(a, kind).start()
        return fields

    def far_end(a, fields):
        for kind in (3, 4, 5):
            far_step(a, kind).wait_recv()
        pair_one = fields[1] + got[a][0].astype(F32)
        quad_sum = fields[2] + got[a][1].astype(F32)
        quad_sum = quad_sum + got[a][2].astype(F32) + got[a][3].astype(F32)
        down = pair_one + mm_t(quad_sum.astype(BF16), transfers[1, odd])
        field = fields[0] + mm_t(down.astype(BF16), transfers[0, core])
        return mm_t(field.astype(BF16), bases[...])

    def far_drain(a):
        for k in range(1, quads):
            far_along(a, k).wait_send()
        for kind in range(6):
            far_step(a, kind).wait_send()

    def operate(e, a):
        far_begin(a, e)
        relay(e, 0)
        relay(e, 1)
        far_mid(a)
        slots(e, 0, near_at, near, "near")
        relay(e, 2)
        slots(e, 1, near_at, near, "near")
        relay(e, 3)
        far_late(a)
        slots(e, 2, near_at, near, "near")
        fields = far_couple(a)
        slots(e, 3, near_at, near, "near")
        return own(e).astype(F32) + acc[...] + far_end(a, fields)

    for c in range(CHUNKS):
        sides_loads[c].wait()
        send_own(0, c)
    blocksum(0, inverse_at, inverse, "inverse")
    first = own(0).astype(F32) + acc[...]
    put_own(1, first)
    sol_ref[...] = first
    put_own(2, own(0).astype(F32) - operate(1, 0))
    blocksum(2, inverse_at, inverse, "inverse")
    second = sol_ref[...] + (own(2).astype(F32) + acc[...])
    put_own(3, second)
    sol_ref[...] = second
    res_ref[...] = own(0).astype(F32) - operate(3, 1)
    for e in range(EXCHANGES):
        drain(e)
    for a in range(2):
        far_drain(a)


def shards(
    count,
    right_sides,
    near_list,
    near_blocks,
    inverse_list,
    inverse_blocks,
    leaf_bases,
    transfers,
    couple_list,
    couple_blocks,
):
    rows, cols = right_sides.shape
    rank = leaf_bases.shape[-1]
    quads = count // 4
    width = cols // CHUNKS
    window = pltpu.VMEM((2 * REACH + 1, rows, width), BF16)
    table = pltpu.VMEM((4, quads, rows, rank), BF16)
    got = pltpu.VMEM((4, rows, rank), BF16)
    mine = pltpu.VMEM((2, rows, rank), BF16)
    dma = pltpu.SemaphoreType.DMA
    loads = near_blocks.shape[1] + inverse_blocks.shape[1] + 3
    scratch = [window] * (EXCHANGES * CHUNKS) + [
        table,
        table,
        got,
        got,
        mine,
        mine,
        pltpu.VMEM((2, quads, rows, rank), BF16),
        pltpu.VMEM((quads, rows, rank), BF16),
        pltpu.VMEM(near_blocks.shape[1:], BF16),
        pltpu.VMEM(inverse_blocks.shape[1:], BF16),
        pltpu.VMEM(leaf_bases.shape[1:], BF16),
        pltpu.VMEM(transfers.shape, BF16),
        pltpu.VMEM(couple_blocks.shape[1:], BF16),
        pltpu.VMEM((rows, cols), F32),
        dma((loads,)),
        dma((CHUNKS,)),
        dma((EXCHANGES, 4, CHUNKS)),
        dma((EXCHANGES, 4, CHUNKS)),
        dma((2, quads)),
        dma((2, quads)),
        dma((2, 6)),
        dma((2, 6)),
    ]
    smem = pl.BlockSpec(memory_space=pltpu.SMEM)
    hbm = pl.BlockSpec(memory_space=pl.ANY)
    vmem = pl.BlockSpec(memory_space=pltpu.VMEM)
    out = jax.ShapeDtypeStruct((rows, cols), F32)
    return pl.pallas_call(
        functools.partial(kernel, count),
        out_shape=(out, out),
        in_specs=[smem] * 3 + [hbm] * 6,
        out_specs=(vmem, vmem),
        scratch_shapes=scratch,
        compiler_params=pltpu.CompilerParams(
            collective_id=0, has_side_effects=True, vmem_limit_bytes=67_043_328
        ),
    )(
        near_list,
        inverse_list,
        jnp.transpose(couple_list, (1, 0, 2)),
        right_sides,
        near_blocks,
        inverse_blocks,
        leaf_bases,
        transfers,
        couple_blocks,
    )


def solution(mesh):
    return jax.shard_map(
        functools.partial(shards, mesh.shape["leaf"]),
        mesh=mesh,
        in_specs=(
            P("parts", "leaf"),
            P(("parts", "leaf"), None),
            P(("parts", "leaf"), None, None, None),
            P(("parts", "leaf"), None),
            P(("parts", "leaf"), None, None, None),
            P(("parts", "leaf"), None, None),
            P(),
            P(("parts", "leaf"), None, None),
            P(("parts", "leaf"), None, None, None, None),
        ),
        out_specs=(P("parts", "leaf"), P("parts", "leaf")),
        check_vma=False,
    )
```

```python
import functools

import jax
import jax.numpy as jnp
from jax import lax
from jax.experimental import pallas as pl
from jax.experimental.pallas import tpu as pltpu
from jax.sharding import PartitionSpec as P

REACH = 2
CHUNKS = 4
EXCHANGES = 4
OWN_SIB, OWN_PAIR, FWD_QUAD, FWD_SIB = range(4)
F32 = jnp.float32
BF16 = jnp.bfloat16


def mm(a, b):
    return jnp.dot(a, b, preferred_element_type=F32)


def mm_t(a, b):
    return lax.dot_general(a, b, (((1,), (1,)), ((), ())), preferred_element_type=F32)


def kernel(
    count,
    near_list,
    inverse_list,
    couple_list,
    sides_hbm,
    near_hbm,
    inverse_hbm,
    bases_hbm,
    transfers_hbm,
    couple_hbm,
    sol_ref,
    res_ref,
    *scratch,
):
    windows = [scratch[e * CHUNKS : (e + 1) * CHUNKS] for e in range(EXCHANGES)]
    (
        tables_a,
        tables_b,
        got_a,
        got_b,
        mine_a,
        mine_b,
        level_one,
        level_two,
        near,
        inverse,
        bases,
        transfers,
        couple,
        acc,
        load_sem,
        sides_sem,
        send_sem,
        recv_sem,
        far_send,
        far_recv,
        row_send,
        row_recv,
        step_send,
        step_recv,
    ) = scratch[EXCHANGES * CHUNKS :]
    tables = (tables_a, tables_b)
    got = (got_a, got_b)
    mine = (mine_a, mine_b)
    quads = count // 4
    rows, cols = sol_ref.shape
    width = cols // CHUNKS

    me = lax.axis_index("leaf")
    core = me % 2
    odd = me // 2 % 2
    member = me % 4
    quad = me // 4
    sibling = me + 1 - 2 * core
    pair = me + 2 - 4 * odd
    across = pair + 1 - 2 * core
    pair_slot = 4 - 4 * odd
    fwd_slot = 4 * odd
    pair_dst_slot = 4 * odd
    fwd_to = me + 4 - 8 * odd
    fwd_out = (fwd_to >= 0) & (fwd_to < count)
    fwd_from = me - 4 + 8 * odd
    fwd_in = (fwd_from >= 0) & (fwd_from < count)
    same = core == odd

    sides_loads = []
    for c in range(CHUNKS):
        load = pltpu.make_async_copy(
            sides_hbm.at[:, pl.ds(c * width, width)], windows[0][c].at[2], sides_sem.at[c]
        )
        load.start()
        sides_loads.append(load)
    loads = {}
    pieces = []
    for s in range(inverse.shape[0]):
        pieces.append(("inverse%d" % s, inverse_hbm.at[0, s], inverse.at[s]))
    pieces.append(("bases", bases_hbm.at[0], bases))
    pieces.append(("transfers", transfers_hbm, transfers))
    pieces.append(("couple", couple_hbm.at[0], couple))
    for s in range(near.shape[0]):
        pieces.append(("near%d" % s, near_hbm.at[0, s], near.at[s]))
    for index, (name, source, target) in enumerate(pieces):
        loads[name] = pltpu.make_async_copy(source, target, load_sem.at[index])
        loads[name].start()

    def wait_load(*names):
        for name in names:
            if name in loads:
                loads.pop(name).wait()

    barrier = pltpu.get_barrier_semaphore()
    partners = [sibling, pair, across]
    partners += [(quad + k) % quads * 4 + member for k in range(1, quads)]
    for other in partners:
        pl.semaphore_signal(
            barrier, inc=1, device_id={"leaf": other}, device_id_type=pl.DeviceIdType.MESH
        )
    pl.semaphore_wait(barrier, len(partners))

    unsent = []

    def remote(src, dst, ssem, rsem, to):
        return pltpu.make_async_remote_copy(
            src_ref=src,
            dst_ref=dst,
            send_sem=ssem,
            recv_sem=rsem,
            device_id={"leaf": to},
            device_id_type=pl.DeviceIdType.MESH,
        )

    def vector_copy(e, c, kind):
        win = windows[e][c]
        if kind == OWN_SIB:
            src, dst, to = 2, 1 + 2 * core, sibling
            dst = jnp.where(core == 0, 1, 3)
        elif kind == OWN_PAIR:
            src, dst, to = 2, pair_dst_slot, pair
        elif kind == FWD_QUAD:
            src, dst, to = pair_slot, fwd_slot, fwd_to
        else:
            src, dst, to = 4 - 4 * core, 3 - 2 * core, sibling
        return remote(
            win.at[src], win.at[dst], send_sem.at[e, kind, c], recv_sem.at[e, kind, c], to
        )

    def start(e, c, kind, pred=None):
        if pred is None:
            vector_copy(e, c, kind).start()
        else:
            pl.when(pred)(lambda: vector_copy(e, c, kind).start())

    def wait_recv(e, c, kind, pred=None):
        if pred is None:
            vector_copy(e, c, kind).wait_recv()
        else:
            pl.when(pred)(lambda: vector_copy(e, c, kind).wait_recv())

    def send_own(e, c):
        start(e, c, OWN_PAIR)
        start(e, c, OWN_SIB)

    def relay(e, c):
        wait_recv(e, c, OWN_PAIR)
        start(e, c, FWD_QUAD, fwd_out)
        start(e, c, FWD_SIB, same)

    def pass_on(e, c):
        wait_recv(e, c, FWD_QUAD, fwd_in)
        start(e, c, FWD_SIB, jnp.logical_not(same) & fwd_in)

    def arrive(e, c):
        wait_recv(e, c, OWN_SIB)
        wait_recv(e, c, FWD_SIB, jnp.logical_not(same) | fwd_in)

    def drain(e):
        for c in range(CHUNKS):
            vector_copy(e, c, OWN_PAIR).wait_send()
            vector_copy(e, c, OWN_SIB).wait_send()
            pl.when(fwd_out)(lambda c=c: vector_copy(e, c, FWD_QUAD).wait_send())
            pl.when(same | fwd_in)(lambda c=c: vector_copy(e, c, FWD_SIB).wait_send())

    def own(e):
        return jnp.concatenate([windows[e][c][2] for c in range(CHUNKS)], axis=1)

    def put_own(e, value):
        for c in range(CHUNKS):
            windows[e][c][2] = value[:, c * width : (c + 1) * width].astype(BF16)
            send_own(e, c)

    def within(leaf):
        return jnp.clip(leaf - me + REACH, 0, 2 * REACH)

    near_at = [within(near_list[0, s]) for s in range(near.shape[0])]
    inverse_at = [within(inverse_list[0, s]) for s in range(inverse.shape[0])]

    def slots(e, c, at, blocks, label):
        arrive(e, c)
        total = None
        for s, position in enumerate(at):
            wait_load("%s%d" % (label, s))
            chosen = windows[e][c][position]
            term = mm(chosen, blocks[s, c * width : (c + 1) * width, :])
            total = term if total is None else total + term
        if c == 0:
            acc[...] = total
        else:
            acc[...] += total

    def blocksum(e, at, blocks, label):
        for c in range(CHUNKS):
            relay(e, c)
        pass_on(e, 0)
        for c in range(CHUNKS):
            if c + 1 < CHUNKS:
                pass_on(e, c + 1)
            slots(e, c, at, blocks, label)

    def far_along(a, k):
        ref = tables[a].at[member, quad]
        return remote(ref, ref, far_send.at[a, k], far_recv.at[a, k], (quad + k) % quads * 4 + member)

    def far_spread(a, kind, k):
        ref = tables[a].at[pair % 4 if kind == 2 else member, (quad - k + quads) % quads]
        to = pair if kind == 0 else sibling
        return remote(ref, ref, row_send.at[a, kind, k], row_recv.at[a, kind, k], to)

    def far_step(a, kind):
        if kind == 0:
            ref, to, dst = mine[a], sibling, got[a].at[pl.ds(0, 2)]
        elif kind == 1:
            ref, to, dst = mine[a].at[1], pair, got[a].at[2]
        else:
            ref, to, dst = mine[a].at[1], across, got[a].at[3]
        return remote(ref, dst, step_send.at[a, kind], step_recv.at[a, kind], to)

    def far_begin(a, e):
        wait_load("bases")
        tables[a][member, quad] = mm(own(e), bases[...]).astype(BF16)
        for k in range(1, quads):
            far_along(a, k).start()
        far_spread(a, 0, 0).start()
        far_spread(a, 1, 0).start()

    def far_mid(a):
        for k in range(1, quads):
            far_along(a, k).wait_recv()
            far_spread(a, 0, k).start()
            far_spread(a, 1, k).start()

    def far_late(a):
        for k in range(quads):
            far_spread(a, 0, k).wait_recv()
            far_spread(a, 2, k).start()

    def far_couple(a):
        table = tables[a]
        wait_load("transfers", "couple")
        for k in range(quads):
            far_spread(a, 1, k).wait_recv()
            far_spread(a, 2, k).wait_recv()
        rank = table.shape[-1]
        flat = (quads * rows, rank)
        for parity in range(2):
            lifted = mm(table[2 * parity].reshape(flat), transfers[0, 0])
            lifted = lifted + mm(table[2 * parity + 1].reshape(flat), transfers[0, 1])
            level_one[parity] = lifted.astype(BF16).reshape(quads, rows, rank)
        lifted = mm(level_one[0].reshape(flat), transfers[1, 0])
        lifted = lifted + mm(level_one[1].reshape(flat), transfers[1, 1])
        level_two[...] = lifted.astype(BF16).reshape(quads, rows, rank)
        fields = []
        for level in range(3):
            total = None
            for k in range(couple.shape[1]):
                at = couple_list[level, 0, k]
                if level == 0:
                    chosen = table[at % 4, at // 4]
                elif level == 1:
                    chosen = level_one[at % 2, at // 2]
                else:
                    chosen = level_two[at]
                term = mm(chosen, couple[level, k])
                total = term if total is None else total + term
            fields.append(total)
        mine[a][0] = fields[1].astype(BF16)
        mine[a][1] = fields[2].astype(BF16)
        for kind in (1, 2, 0):
            far_step(a, kind).start()
        return fields

    def far_end(a, fields):
        for kind in (0, 1, 2):
            far_step(a, kind).wait_recv()
        pair_one = fields[1] + got[a][0].astype(F32)
        quad_sum = fields[2] + got[a][1].astype(F32)
        quad_sum = quad_sum + got[a][2].astype(F32) + got[a][3].astype(F32)
        down = pair_one + mm_t(quad_sum.astype(BF16), transfers[1, odd])
        field = fields[0] + mm_t(down.astype(BF16), transfers[0, core])
        return mm_t(field.astype(BF16), bases[...])

    def far_drain(a):
        for k in range(1, quads):
            far_along(a, k).wait_send()
        for kind in range(3):
            far_step(a, kind).wait_send()
            for k in range(quads):
                far_spread(a, kind, k).wait_send()

    def operate(e, a):
        far_begin(a, e)
        for c in range(CHUNKS - 1):
            relay(e, c)
        far_mid(a)
        relay(e, CHUNKS - 1)
        for c in range(CHUNKS - 1):
            pass_on(e, c)
            if c + 1 == CHUNKS // 2:
                far_late(a)
        for c in range(CHUNKS - 1):
            slots(e, c, near_at, near, "near")
        pass_on(e, CHUNKS - 1)
        fields = far_couple(a)
        slots(e, CHUNKS - 1, near_at, near, "near")
        return own(e).astype(F32) + acc[...] + far_end(a, fields)

    for c in range(CHUNKS):
        sides_loads[c].wait()
        send_own(0, c)
    blocksum(0, inverse_at, inverse, "inverse")
    first = own(0).astype(F32) + acc[...]
    put_own(1, first)
    sol_ref[...] = first
    put_own(2, own(0).astype(F32) - operate(1, 0))
    blocksum(2, inverse_at, inverse, "inverse")
    second = sol_ref[...] + (own(2).astype(F32) + acc[...])
    put_own(3, second)
    sol_ref[...] = second
    res_ref[...] = own(0).astype(F32) - operate(3, 1)
    for e in range(EXCHANGES):
        drain(e)
    for a in range(2):
        far_drain(a)


def shards(
    count,
    right_sides,
    near_list,
    near_blocks,
    inverse_list,
    inverse_blocks,
    leaf_bases,
    transfers,
    couple_list,
    couple_blocks,
):
    rows, cols = right_sides.shape
    rank = leaf_bases.shape[-1]
    quads = count // 4
    width = cols // CHUNKS
    window = pltpu.VMEM((2 * REACH + 1, rows, width), BF16)
    table = pltpu.VMEM((4, quads, rows, rank), BF16)
    got = pltpu.VMEM((4, rows, rank), BF16)
    mine = pltpu.VMEM((2, rows, rank), BF16)
    dma = pltpu.SemaphoreType.DMA
    loads = near_blocks.shape[1] + inverse_blocks.shape[1] + 3
    scratch = [window] * (EXCHANGES * CHUNKS) + [
        table,
        table,
        got,
        got,
        mine,
        mine,
        pltpu.VMEM((2, quads, rows, rank), BF16),
        pltpu.VMEM((quads, rows, rank), BF16),
        pltpu.VMEM(near_blocks.shape[1:], BF16),
        pltpu.VMEM(inverse_blocks.shape[1:], BF16),
        pltpu.VMEM(leaf_bases.shape[1:], BF16),
        pltpu.VMEM(transfers.shape, BF16),
        pltpu.VMEM(couple_blocks.shape[1:], BF16),
        pltpu.VMEM((rows, cols), F32),
        dma((loads,)),
        dma((CHUNKS,)),
        dma((EXCHANGES, 4, CHUNKS)),
        dma((EXCHANGES, 4, CHUNKS)),
        dma((2, quads)),
        dma((2, quads)),
        dma((2, 3, quads)),
        dma((2, 3, quads)),
        dma((2, 3)),
        dma((2, 3)),
    ]
    smem = pl.BlockSpec(memory_space=pltpu.SMEM)
    hbm = pl.BlockSpec(memory_space=pl.ANY)
    vmem = pl.BlockSpec(memory_space=pltpu.VMEM)
    out = jax.ShapeDtypeStruct((rows, cols), F32)
    return pl.pallas_call(
        functools.partial(kernel, count),
        out_shape=(out, out),
        in_specs=[smem] * 3 + [hbm] * 6,
        out_specs=(vmem, vmem),
        scratch_shapes=scratch,
        compiler_params=pltpu.CompilerParams(
            collective_id=0, has_side_effects=True, vmem_limit_bytes=67_043_328
        ),
    )(
        near_list,
        inverse_list,
        jnp.transpose(couple_list, (1, 0, 2)),
        right_sides,
        near_blocks,
        inverse_blocks,
        leaf_bases,
        transfers,
        couple_blocks,
    )


def solution(mesh):
    return jax.shard_map(
        functools.partial(shards, mesh.shape["leaf"]),
        mesh=mesh,
        in_specs=(
            P("parts", "leaf"),
            P(("parts", "leaf"), None),
            P(("parts", "leaf"), None, None, None),
            P(("parts", "leaf"), None),
            P(("parts", "leaf"), None, None, None),
            P(("parts", "leaf"), None, None),
            P(),
            P(("parts", "leaf"), None, None),
            P(("parts", "leaf"), None, None, None, None),
        ),
        out_specs=(P("parts", "leaf"), P("parts", "leaf")),
        check_vma=False,
    )
```

```python
import functools

import jax
import jax.numpy as jnp
from jax import lax
from jax.experimental import pallas as pl
from jax.experimental.pallas import tpu as pltpu
from jax.sharding import PartitionSpec as P

REACH = 2
CHUNKS = 4
EXCHANGES = 4
OWN_SIB, OWN_PAIR, FWD_QUAD, FWD_SIB = range(4)
F32 = jnp.float32
BF16 = jnp.bfloat16


def mm(a, b):
    return jnp.dot(a, b, preferred_element_type=F32)


def mm_t(a, b):
    return lax.dot_general(a, b, (((1,), (1,)), ((), ())), preferred_element_type=F32)


def kernel(
    count,
    near_list,
    inverse_list,
    couple_list,
    sides_hbm,
    near_hbm,
    inverse_hbm,
    bases_hbm,
    transfers_hbm,
    couple_hbm,
    sol_ref,
    res_ref,
    *scratch,
):
    windows = [scratch[e * CHUNKS : (e + 1) * CHUNKS] for e in range(EXCHANGES)]
    (
        tables_a,
        tables_b,
        got_a,
        got_b,
        mine_a,
        mine_b,
        level_one,
        level_two,
        near,
        inverse,
        bases,
        transfers,
        couple,
        acc,
        load_sem,
        sides_sem,
        send_sem,
        recv_sem,
        far_send,
        far_recv,
        row_send,
        row_recv,
        step_send,
        step_recv,
    ) = scratch[EXCHANGES * CHUNKS :]
    tables = (tables_a, tables_b)
    got = (got_a, got_b)
    mine = (mine_a, mine_b)
    quads = count // 4
    rows, cols = sol_ref.shape
    width = cols // CHUNKS

    me = lax.axis_index("leaf")
    core = me % 2
    odd = me // 2 % 2
    member = me % 4
    quad = me // 4
    sibling = me + 1 - 2 * core
    pair = me + 2 - 4 * odd
    across = pair + 1 - 2 * core
    pair_slot = 4 - 4 * odd
    fwd_slot = 4 * odd
    pair_dst_slot = 4 * odd
    fwd_to = me + 4 - 8 * odd
    fwd_out = (fwd_to >= 0) & (fwd_to < count)
    fwd_from = me - 4 + 8 * odd
    fwd_in = (fwd_from >= 0) & (fwd_from < count)
    same = core == odd

    sides_loads = []
    for c in range(CHUNKS):
        load = pltpu.make_async_copy(
            sides_hbm.at[:, pl.ds(c * width, width)], windows[0][c].at[2], sides_sem.at[c]
        )
        load.start()
        sides_loads.append(load)
    loads = {}
    pieces = []
    for s in range(inverse.shape[0]):
        pieces.append(("inverse%d" % s, inverse_hbm.at[0, s], inverse.at[s]))
    pieces.append(("bases", bases_hbm.at[0], bases))
    pieces.append(("transfers", transfers_hbm, transfers))
    pieces.append(("couple", couple_hbm.at[0], couple))
    for s in range(near.shape[0]):
        pieces.append(("near%d" % s, near_hbm.at[0, s], near.at[s]))
    for index, (name, source, target) in enumerate(pieces):
        loads[name] = pltpu.make_async_copy(source, target, load_sem.at[index])
        loads[name].start()

    def wait_load(*names):
        for name in names:
            if name in loads:
                loads.pop(name).wait()

    barrier = pltpu.get_barrier_semaphore()
    partners = [sibling, pair, across]
    partners += [(quad + k) % quads * 4 + member for k in range(1, quads)]
    for other in partners:
        pl.semaphore_signal(
            barrier, inc=1, device_id={"leaf": other}, device_id_type=pl.DeviceIdType.MESH
        )
    pl.semaphore_wait(barrier, len(partners))

    unsent = []

    def remote(src, dst, ssem, rsem, to):
        return pltpu.make_async_remote_copy(
            src_ref=src,
            dst_ref=dst,
            send_sem=ssem,
            recv_sem=rsem,
            device_id={"leaf": to},
            device_id_type=pl.DeviceIdType.MESH,
        )

    def vector_copy(e, c, kind):
        win = windows[e][c]
        if kind == OWN_SIB:
            src, dst, to = 2, 1 + 2 * core, sibling
            dst = jnp.where(core == 0, 1, 3)
        elif kind == OWN_PAIR:
            src, dst, to = 2, pair_dst_slot, pair
        elif kind == FWD_QUAD:
            src, dst, to = pair_slot, fwd_slot, fwd_to
        else:
            src, dst, to = 4 - 4 * core, 3 - 2 * core, sibling
        return remote(
            win.at[src], win.at[dst], send_sem.at[e, kind, c], recv_sem.at[e, kind, c], to
        )

    def start(e, c, kind, pred=None):
        if pred is None:
            vector_copy(e, c, kind).start()
        else:
            pl.when(pred)(lambda: vector_copy(e, c, kind).start())

    def wait_recv(e, c, kind, pred=None):
        if pred is None:
            vector_copy(e, c, kind).wait_recv()
        else:
            pl.when(pred)(lambda: vector_copy(e, c, kind).wait_recv())

    def send_own(e, c):
        start(e, c, OWN_PAIR)
        start(e, c, OWN_SIB)

    def relay(e, c):
        wait_recv(e, c, OWN_PAIR)
        start(e, c, FWD_QUAD, fwd_out)
        start(e, c, FWD_SIB, same)

    def pass_on(e, c):
        wait_recv(e, c, FWD_QUAD, fwd_in)
        start(e, c, FWD_SIB, jnp.logical_not(same) & fwd_in)

    def arrive(e, c):
        wait_recv(e, c, OWN_SIB)
        wait_recv(e, c, FWD_SIB, jnp.logical_not(same) | fwd_in)

    def drain(e):
        for c in range(CHUNKS):
            vector_copy(e, c, OWN_PAIR).wait_send()
            vector_copy(e, c, OWN_SIB).wait_send()
            pl.when(fwd_out)(lambda c=c: vector_copy(e, c, FWD_QUAD).wait_send())
            pl.when(same | fwd_in)(lambda c=c: vector_copy(e, c, FWD_SIB).wait_send())

    def own(e):
        return jnp.concatenate([windows[e][c][2] for c in range(CHUNKS)], axis=1)

    def put_own(e, value):
        for c in range(CHUNKS):
            windows[e][c][2] = value[:, c * width : (c + 1) * width].astype(BF16)
            send_own(e, c)

    def within(leaf):
        return jnp.clip(leaf - me + REACH, 0, 2 * REACH)

    near_at = [within(near_list[0, s]) for s in range(near.shape[0])]
    inverse_at = [within(inverse_list[0, s]) for s in range(inverse.shape[0])]

    def slots(e, c, at, blocks, label):
        arrive(e, c)
        total = None
        for s, position in enumerate(at):
            wait_load("%s%d" % (label, s))
            chosen = windows[e][c][position]
            term = mm(chosen, blocks[s, c * width : (c + 1) * width, :])
            total = term if total is None else total + term
        if c == 0:
            acc[...] = total
        else:
            acc[...] += total

    def blocksum(e, at, blocks, label):
        for c in range(CHUNKS):
            relay(e, c)
        pass_on(e, 0)
        for c in range(CHUNKS):
            if c + 1 < CHUNKS:
                pass_on(e, c + 1)
            slots(e, c, at, blocks, label)

    def far_along(a, k):
        ref = tables[a].at[member, quad]
        return remote(ref, ref, far_send.at[a, k], far_recv.at[a, k], (quad + k) % quads * 4 + member)

    def far_spread(a, kind, k):
        ref = tables[a].at[pair % 4 if kind == 2 else member, (quad - k + quads) % quads]
        to = pair if kind == 0 else sibling
        return remote(ref, ref, row_send.at[a, kind, k], row_recv.at[a, kind, k], to)

    def far_step(a, kind):
        if kind == 0:
            ref, to, dst = mine[a], sibling, got[a].at[pl.ds(0, 2)]
        elif kind == 1:
            ref, to, dst = mine[a].at[1], pair, got[a].at[2]
        else:
            ref, to, dst = mine[a].at[1], across, got[a].at[3]
        return remote(ref, dst, step_send.at[a, kind], step_recv.at[a, kind], to)

    def far_begin(a, e):
        wait_load("bases")
        tables[a][member, quad] = mm(own(e), bases[...]).astype(BF16)
        for k in range(1, quads):
            far_along(a, k).start()
        far_spread(a, 0, 0).start()
        far_spread(a, 1, 0).start()

    def far_mid(a):
        for k in range(1, quads):
            far_along(a, k).wait_recv()
            far_spread(a, 0, k).start()
            far_spread(a, 1, k).start()

    def far_late(a):
        for k in range(quads):
            far_spread(a, 0, k).wait_recv()
            far_spread(a, 2, k).start()

    def far_couple(a):
        table = tables[a]
        wait_load("transfers", "couple")
        for k in range(quads):
            far_spread(a, 1, k).wait_recv()
            far_spread(a, 2, k).wait_recv()
        rank = table.shape[-1]
        flat = (quads * rows, rank)
        for parity in range(2):
            lifted = mm(table[2 * parity].reshape(flat), transfers[0, 0])
            lifted = lifted + mm(table[2 * parity + 1].reshape(flat), transfers[0, 1])
            level_one[parity] = lifted.astype(BF16).reshape(quads, rows, rank)
        lifted = mm(level_one[0].reshape(flat), transfers[1, 0])
        lifted = lifted + mm(level_one[1].reshape(flat), transfers[1, 1])
        level_two[...] = lifted.astype(BF16).reshape(quads, rows, rank)
        fields = []
        for level in range(3):
            total = None
            for k in range(couple.shape[1]):
                at = couple_list[level, 0, k]
                if level == 0:
                    chosen = table[at % 4, at // 4]
                elif level == 1:
                    chosen = level_one[at % 2, at // 2]
                else:
                    chosen = level_two[at]
                term = mm(chosen, couple[level, k])
                total = term if total is None else total + term
            fields.append(total)
        mine[a][0] = fields[1].astype(BF16)
        mine[a][1] = fields[2].astype(BF16)
        for kind in (1, 2, 0):
            far_step(a, kind).start()
        return fields

    def far_end(a, fields):
        for kind in (0, 1, 2):
            far_step(a, kind).wait_recv()
        pair_one = fields[1] + got[a][0].astype(F32)
        quad_sum = fields[2] + got[a][1].astype(F32)
        quad_sum = quad_sum + got[a][2].astype(F32) + got[a][3].astype(F32)
        down = pair_one + mm_t(quad_sum.astype(BF16), transfers[1, odd])
        field = fields[0] + mm_t(down.astype(BF16), transfers[0, core])
        return mm_t(field.astype(BF16), bases[...])

    def far_drain(a):
        for k in range(1, quads):
            far_along(a, k).wait_send()
        for kind in range(3):
            far_step(a, kind).wait_send()
            for k in range(quads):
                far_spread(a, kind, k).wait_send()

    def operate(e, a):
        far_begin(a, e)
        for c in range(CHUNKS // 2):
            relay(e, c)
        far_mid(a)
        for c in range(CHUNKS // 2, CHUNKS):
            relay(e, c)
        for c in range(CHUNKS - 1):
            pass_on(e, c)
            if c + 1 == CHUNKS // 2:
                far_late(a)
        for c in range(CHUNKS // 2):
            slots(e, c, near_at, near, "near")
        pass_on(e, CHUNKS - 1)
        fields = far_couple(a)
        for c in range(CHUNKS // 2, CHUNKS):
            slots(e, c, near_at, near, "near")
        return own(e).astype(F32) + acc[...] + far_end(a, fields)

    for c in range(CHUNKS):
        sides_loads[c].wait()
        send_own(0, c)
    blocksum(0, inverse_at, inverse, "inverse")
    first = own(0).astype(F32) + acc[...]
    put_own(1, first)
    sol_ref[...] = first
    put_own(2, own(0).astype(F32) - operate(1, 0))
    blocksum(2, inverse_at, inverse, "inverse")
    second = sol_ref[...] + (own(2).astype(F32) + acc[...])
    put_own(3, second)
    sol_ref[...] = second
    res_ref[...] = own(0).astype(F32) - operate(3, 1)
    for e in range(EXCHANGES):
        drain(e)
    for a in range(2):
        far_drain(a)


def shards(
    count,
    right_sides,
    near_list,
    near_blocks,
    inverse_list,
    inverse_blocks,
    leaf_bases,
    transfers,
    couple_list,
    couple_blocks,
):
    rows, cols = right_sides.shape
    rank = leaf_bases.shape[-1]
    quads = count // 4
    width = cols // CHUNKS
    window = pltpu.VMEM((2 * REACH + 1, rows, width), BF16)
    table = pltpu.VMEM((4, quads, rows, rank), BF16)
    got = pltpu.VMEM((4, rows, rank), BF16)
    mine = pltpu.VMEM((2, rows, rank), BF16)
    dma = pltpu.SemaphoreType.DMA
    loads = near_blocks.shape[1] + inverse_blocks.shape[1] + 3
    scratch = [window] * (EXCHANGES * CHUNKS) + [
        table,
        table,
        got,
        got,
        mine,
        mine,
        pltpu.VMEM((2, quads, rows, rank), BF16),
        pltpu.VMEM((quads, rows, rank), BF16),
        pltpu.VMEM(near_blocks.shape[1:], BF16),
        pltpu.VMEM(inverse_blocks.shape[1:], BF16),
        pltpu.VMEM(leaf_bases.shape[1:], BF16),
        pltpu.VMEM(transfers.shape, BF16),
        pltpu.VMEM(couple_blocks.shape[1:], BF16),
        pltpu.VMEM((rows, cols), F32),
        dma((loads,)),
        dma((CHUNKS,)),
        dma((EXCHANGES, 4, CHUNKS)),
        dma((EXCHANGES, 4, CHUNKS)),
        dma((2, quads)),
        dma((2, quads)),
        dma((2, 3, quads)),
        dma((2, 3, quads)),
        dma((2, 3)),
        dma((2, 3)),
    ]
    smem = pl.BlockSpec(memory_space=pltpu.SMEM)
    hbm = pl.BlockSpec(memory_space=pl.ANY)
    vmem = pl.BlockSpec(memory_space=pltpu.VMEM)
    out = jax.ShapeDtypeStruct((rows, cols), F32)
    return pl.pallas_call(
        functools.partial(kernel, count),
        out_shape=(out, out),
        in_specs=[smem] * 3 + [hbm] * 6,
        out_specs=(vmem, vmem),
        scratch_shapes=scratch,
        compiler_params=pltpu.CompilerParams(
            collective_id=0, has_side_effects=True, vmem_limit_bytes=67_043_328
        ),
    )(
        near_list,
        inverse_list,
        jnp.transpose(couple_list, (1, 0, 2)),
        right_sides,
        near_blocks,
        inverse_blocks,
        leaf_bases,
        transfers,
        couple_blocks,
    )


def solution(mesh):
    return jax.shard_map(
        functools.partial(shards, mesh.shape["leaf"]),
        mesh=mesh,
        in_specs=(
            P("parts", "leaf"),
            P(("parts", "leaf"), None),
            P(("parts", "leaf"), None, None, None),
            P(("parts", "leaf"), None),
            P(("parts", "leaf"), None, None, None),
            P(("parts", "leaf"), None, None),
            P(),
            P(("parts", "leaf"), None, None),
            P(("parts", "leaf"), None, None, None, None),
        ),
        out_specs=(P("parts", "leaf"), P("parts", "leaf")),
        check_vma=False,
    )
```
